32 devices in a mesh: shard: 4 (over y, x), rep: 8 (over z, core).
Axes of the slice: x: 2, y: 2, z: 4, core: 2. Of those that a mesh axis runs over, the one named last changes fastest.
Arguments:
- layer_in: float32 [4096, 960], P(('shard', 'rep')), may hold values from -6 to 6
- segments: int32 [4096], P(('shard', 'rep')), may hold values from 0 to 15, as said below
- cotangent: float32 [4096, 960], P(('shard', 'rep')), may hold values from -6 to 6
- w_query: bfloat16 [960, 960], P('shard'), may hold values from -0.1875 to 0.1875
- key_matrix: bfloat16 [960, 320], P('shard'), may hold values from -0.1875 to 0.1875
- value_matrix: bfloat16 [960, 320], P('shard'), may hold values from -0.1875 to 0.1875
- output_matrix: bfloat16 [960, 960], P(None, 'shard'), may hold values from -0.75 to 0.75
- gain_attn: bfloat16 [960], P('shard'), may hold values from 0.5 to 1.5
- w_gate: bfloat16 [960, 2560], P('shard'), may hold values from -0.1875 to 0.1875
- w_up: bfloat16 [960, 2560], P('shard'), may hold values from -0.1875 to 0.1875
- w_down: bfloat16 [2560, 960], P(None, 'shard'), may hold values from -0.125 to 0.125
- gain_ffn: bfloat16 [960], P('shard'), may hold values from 0.5 to 1.5
Outputs:
- layer_out: float32 [4096, 960], P(('shard', 'rep'))
- input_grad: float32 [4096, 960], P(('shard', 'rep'))
- grad_query: float32 [960, 960], P('shard')
- grad_key: float32 [960, 320], P('shard')
- grad_value: float32 [960, 320], P('shard')
- grad_output: float32 [960, 960], P(None, 'shard')
- grad_gain_attn: float32 [960], P('shard')
- grad_gate: float32 [960, 2560], P('shard')
- grad_up: float32 [960, 2560], P('shard')
- grad_down: float32 [2560, 960], P(None, 'shard')
- grad_gain_ffn: float32 [960], P('shard')
The draws below stay inside these ranges and needn't reach their ends.
Inputs may be any that keep to these rules, and one draw needn't show every extreme that they name: `segments`: within each device's 128 slots the value starts at 0 and rises by 0 or 1 from slot to slot; every document lies in one device's slots; a device holds at most 16 documents.
All inputs are finite; a program needn't handle non-finite values.
Results may differ from the reference program's by a relative error of at most 0.012.
Values may be sent and summed in bfloat16 or wider, within the bound.
No kernel may reach another device: no remote copies, remote signals or barrier semaphores. Data moves between devices by JAX's collectives and lax.ppermute only.
A program may use at most 192 MiB of HBM per device.

```python
import jax
import jax.numpy as jnp
from jax import lax

D = 960
FF = 2560
QUERY_HEADS = 15
KEY_VALUE_HEADS = 5
HEAD_WIDTH = 64
TOK_DEV = 128
QD = 960
KD = 320
TOKENS = 4096


def draw_segments(key, part):
    blocks = TOKENS // TOK_DEV
    key_flags = jax.random.fold_in(key, 11)
    key_pick = jax.random.fold_in(key, 23)
    flags = jax.random.randint(key_flags, (blocks, TOK_DEV), 0, max(TOK_DEV // 4, 2)) == 0
    index = jnp.arange(TOK_DEV, dtype=jnp.int32)
    chosen = jax.random.randint(key_pick, (), 0, blocks)
    forced = (jnp.arange(blocks, dtype=jnp.int32)[:, None] == chosen) & (index[None, :] % 8 == 0)
    first = index[None, :] == 0
    flags = jnp.logical_or(jnp.logical_or(flags, first), forced).astype(jnp.int32)
    ids = jnp.cumsum(flags, axis=1) - 1
    ids = jnp.minimum(ids, TOK_DEV // 8 - 1)
    return ids.astype(jnp.int32).reshape(TOKENS)


def level_of(key, shape, pieces, low, largest):
    def one(dim, shards_of):
        heights = jax.random.uniform(jax.random.fold_in(jax.random.fold_in(key, 6), dim), (shards_of,), jnp.float32, low / len(pieces), largest / len(pieces))
        return jnp.repeat(jnp.exp(heights), shape[dim] // shards_of).reshape((-1,) + (1,) * (len(shape) - dim - 1))

    loudness = one(*pieces[0])
    for cut in pieces[1:]:
        loudness = loudness * one(*cut)
    return loudness


def gaussian(stream_key, extent, deviation, most, cuts=(), kind=jnp.bfloat16):
    array = deviation * jax.random.normal(stream_key, extent, jnp.float32)
    if cuts:
        array = array * level_of(stream_key, extent, cuts, -0.22, 0.18)
    return jnp.clip(array, -most, most).astype(kind)


def setup_inputs(seed: int = 0) -> dict:
    key_list = jax.random.split(jax.random.key(seed), 13)
    return {
        "layer_in": gaussian(key_list[0], (TOKENS, D), 1.0, 6.0, ((0, 32),), jnp.float32),
        "segments": draw_segments(jax.random.fold_in(key_list[12], 71), 0),
        "cotangent": gaussian(key_list[2], (TOKENS, D), 1.0, 6.0, ((0, 32),), jnp.float32),
        "w_query": gaussian(key_list[3], (D, QD), D ** -0.5, 0.1875, ((0, 4),)),
        "key_matrix": gaussian(key_list[4], (D, KD), D ** -0.5, 0.1875, ((0, 4),)),
        "value_matrix": gaussian(key_list[5], (D, KD), D ** -0.5, 0.1875, ((0, 4),)),
        "output_matrix": gaussian(key_list[6], (QD, D), (QD // 16) ** -0.5, 0.75, ((1, 4),)),
        "gain_attn": jnp.clip(1.0 + 0.1 * jax.random.normal(key_list[7], (D,), jnp.float32), 0.5, 1.5).astype(jnp.bfloat16),
        "w_gate": gaussian(key_list[8], (D, FF), D ** -0.5, 0.1875, ((0, 4),)),
        "w_up": gaussian(key_list[9], (D, FF), D ** -0.5, 0.1875, ((0, 4),)),
        "w_down": gaussian(key_list[10], (FF, D), FF ** -0.5, 0.125, ((1, 4),)),
        "gain_ffn": jnp.clip(1.0 + 0.1 * jax.random.normal(key_list[11], (D,), jnp.float32), 0.5, 1.5).astype(jnp.bfloat16),
    }


EPS = 1e-05
THETA = 10000.0

def matmul_plain(left, right):
    return jnp.dot(left, right, preferred_element_type=jnp.float32)

def matmul_transposed(left, right):
    return lax.dot_general(left, right, (((1,), (1,)), ((), ())), preferred_element_type=jnp.float32)

def dot_tn(left, right):
    return lax.dot_general(left, right, (((0,), (0,)), ((), ())), preferred_element_type=jnp.float32)

def mixing(form, left, right):
    return jnp.einsum(form, left.astype(jnp.float32), right.astype(jnp.float32))

def tables(segs):
    token_count = segs.shape[0]
    index = jnp.arange(token_count, dtype=jnp.int32)
    start = lax.optimization_barrier(jnp.sum((segs[None, :] < segs[:, None]).astype(jnp.int32), axis=1))
    posit = (index - start).astype(jnp.float32)
    half = HEAD_WIDTH // 2
    inverse = THETA ** (-(2.0 * jnp.arange(half, dtype=jnp.float32)) / HEAD_WIDTH)
    angle = posit[:, None] * inverse[None, :]
    visible = (segs[:, None] == segs[None, :]) & (index[:, None] >= index[None, :])
    return (jnp.cos(angle), jnp.sin(angle), visible)

def apply_rotary(tensor, cosine_table, sine_table, sign):
    half = tensor.shape[-1] // 2
    first = tensor[..., :half]
    second = tensor[..., half:]
    cos_b = cosine_table[:, None, :]
    sin_b = sine_table[:, None, :] * sign
    return jnp.concatenate([first * cos_b - second * sin_b, second * cos_b + first * sin_b], axis=-1)

def norm_fwd(rows, gain):
    recip = lax.rsqrt(lax.optimization_barrier(jnp.mean(rows * rows, axis=1, keepdims=True)) + EPS)
    normal = rows * recip
    return ((normal * gain.astype(jnp.float32)).astype(jnp.bfloat16), normal, recip)

def norm_bwd(upper, normal, recip, gain):
    dgain = lax.optimization_barrier(jnp.sum(upper * normal, axis=0))
    scaled = upper * gain.astype(jnp.float32)
    return (dgain, recip * (scaled - normal * lax.optimization_barrier(jnp.mean(scaled * normal, axis=1, keepdims=True))))

def scores(query_rows, key_rows, visible):
    raw = mixing('qhgd,khd->hgqk', query_rows, key_rows) * HEAD_WIDTH ** (-0.5)
    return jnp.where(visible[None, None], raw, -1e+30)

def layer(xrows, segs, cotan, w_query, key_matrix, value_matrix, output_matrix, gain_attn, w_gate, w_up, w_down, gain_ffn):
    token_count = xrows.shape[0]
    cosine_table, sine_table, visible = tables(segs)
    attention_normed1, xn1, recip1 = norm_fwd(xrows, gain_attn)
    query_rows = apply_rotary(matmul_plain(attention_normed1, w_query).reshape(token_count, QUERY_HEADS, HEAD_WIDTH), cosine_table, sine_table, 1.0)
    query_rows = query_rows.reshape(token_count, KEY_VALUE_HEADS, QUERY_HEADS // KEY_VALUE_HEADS, HEAD_WIDTH).astype(jnp.bfloat16)
    key_rows = apply_rotary(matmul_plain(attention_normed1, key_matrix).reshape(token_count, KEY_VALUE_HEADS, HEAD_WIDTH), cosine_table, sine_table, 1.0).astype(jnp.bfloat16)
    value_rows = matmul_plain(attention_normed1, value_matrix).reshape(token_count, KEY_VALUE_HEADS, HEAD_WIDTH).astype(jnp.bfloat16)
    logits = scores(query_rows, key_rows, visible)
    peak = lax.optimization_barrier(jnp.max(logits, axis=-1))
    lse = peak + jnp.log(lax.optimization_barrier(jnp.sum(jnp.exp(logits - peak[..., None]), axis=-1)))
    probs = jnp.exp(logits - lse[..., None]).astype(jnp.bfloat16)
    attn = mixing('hgqk,khd->qhgd', probs, value_rows).reshape(token_count, QUERY_HEADS * HEAD_WIDTH).astype(jnp.bfloat16)
    mid = xrows + matmul_plain(attn, output_matrix)
    normed2, xn2, recip2 = norm_fwd(mid, gain_ffn)
    gate = matmul_plain(normed2, w_gate)
    upval = matmul_plain(normed2, w_up)
    sigm = jax.nn.sigmoid(gate)
    silu = gate * sigm
    hidden = (silu * upval).astype(jnp.bfloat16)
    result = mid + matmul_plain(hidden, w_down)
    dout = cotan.astype(jnp.bfloat16)
    g_down = dot_tn(hidden, dout)
    dhid = matmul_transposed(dout, w_down)
    dgate = (dhid * upval * sigm * (1.0 + gate * (1.0 - sigm))).astype(jnp.bfloat16)
    dup = (dhid * silu).astype(jnp.bfloat16)
    g_gate = dot_tn(normed2, dgate)
    g_up = dot_tn(normed2, dup)
    dn2 = matmul_transposed(dgate, w_gate) + matmul_transposed(dup, w_up)
    g_gain2, dmid_n = norm_bwd(dn2, xn2, recip2, gain_ffn)
    dmid = cotan + dmid_n
    middle_gradient_batch = dmid.astype(jnp.bfloat16)
    g_output = dot_tn(attn, middle_gradient_batch)
    attention_gradient = matmul_transposed(middle_gradient_batch, output_matrix).astype(jnp.bfloat16).reshape(token_count, KEY_VALUE_HEADS, QUERY_HEADS // KEY_VALUE_HEADS, HEAD_WIDTH)
    prob32 = jnp.exp(logits - lse[..., None])
    probs_b = prob32.astype(jnp.bfloat16)
    value_gradient = mixing('hgqk,qhgd->khd', probs_b, attention_gradient)
    dprob = mixing('qhgd,khd->hgqk', attention_gradient, value_rows)
    delta = lax.optimization_barrier(jnp.sum(prob32 * dprob, axis=-1))
    dscore = (prob32 * (dprob - delta[..., None]) * HEAD_WIDTH ** (-0.5)).astype(jnp.bfloat16)
    dquery = mixing('hgqk,khd->qhgd', dscore, key_rows).reshape(token_count, QUERY_HEADS, HEAD_WIDTH)
    key_gradient = mixing('hgqk,qhgd->khd', dscore, query_rows)
    dqr = apply_rotary(dquery, cosine_table, sine_table, -1.0).reshape(token_count, QUERY_HEADS * HEAD_WIDTH).astype(jnp.bfloat16)
    rotated_key_gradient = apply_rotary(key_gradient, cosine_table, sine_table, -1.0).reshape(token_count, KEY_VALUE_HEADS * HEAD_WIDTH).astype(jnp.bfloat16)
    repeated_value_gradient = value_gradient.reshape(token_count, KEY_VALUE_HEADS * HEAD_WIDTH).astype(jnp.bfloat16)
    g_query = dot_tn(attention_normed1, dqr)
    g_key = dot_tn(attention_normed1, rotated_key_gradient)
    g_value = dot_tn(attention_normed1, repeated_value_gradient)
    dn1 = matmul_transposed(dqr, w_query) + matmul_transposed(rotated_key_gradient, key_matrix) + matmul_transposed(repeated_value_gradient, value_matrix)
    g_gain1, dx_n = norm_bwd(dn1, xn1, recip1, gain_attn)
    return (result, dmid + dx_n, (g_query, g_key, g_value, g_output, g_gain1, g_gate, g_up, g_down, g_gain2))

def reference(layer_in, segments, cotangent, w_query, key_matrix, value_matrix, output_matrix, gain_attn, w_gate, w_up, w_down, gain_ffn):
    blocks = layer_in.shape[0] // TOK_DEV
    row_blocks = layer_in.reshape(blocks, TOK_DEV, D)
    seg_blocks = segments.reshape(blocks, TOK_DEV)
    cot_blocks = cotangent.reshape(blocks, TOK_DEV, D)
    shapes = (w_query, key_matrix, value_matrix, output_matrix, gain_attn, w_gate, w_up, w_down, gain_ffn)
    initial = tuple((jnp.zeros(entry.shape, jnp.float32) for entry in shapes))

    def advance(carry, entry):
        xrows, segs, cotan = entry
        result, dxrows, grads = layer(xrows, segs, cotan, w_query, key_matrix, value_matrix, output_matrix, gain_attn, w_gate, w_up, w_down, gain_ffn)
        return (tuple((total + piece for total, piece in zip(carry, grads))), (result, dxrows))
    totals, (results, grad_rows) = lax.scan(advance, initial, (row_blocks, seg_blocks, cot_blocks))
    return (results.reshape(-1, D), grad_rows.reshape(-1, D), totals[0], totals[1], totals[2], totals[3], totals[4], totals[5], totals[6], totals[7], totals[8])
```

```python
import jax
import jax.numpy as jnp
from jax import lax
from jax.sharding import PartitionSpec as P

QUERY_HEADS = 15
KEY_VALUE_HEADS = 5
HEAD_WIDTH = 64

EPS = 1e-05
THETA = 10000.0
BF = jnp.bfloat16
F32 = jnp.float32


def matmul_plain(left, right):
    return jnp.dot(left, right, preferred_element_type=F32)


def matmul_transposed(left, right):
    return lax.dot_general(left, right, (((1,), (1,)), ((), ())), preferred_element_type=F32)


def dot_tn(left, right):
    return lax.dot_general(left, right, (((0,), (0,)), ((), ())), preferred_element_type=F32)


def mixing(form, left, right):
    return jnp.einsum(form, left, right, preferred_element_type=F32)


def tables(segs, head_size):
    token_count = segs.shape[0]
    index = jnp.arange(token_count, dtype=jnp.int32)
    start = jnp.sum((segs[None, :] < segs[:, None]).astype(jnp.int32), axis=1)
    posit = (index - start).astype(F32)
    half = head_size // 2
    inverse = THETA ** (-(2.0 * jnp.arange(half, dtype=F32)) / head_size)
    angle = posit[:, None] * inverse[None, :]
    visible = (segs[:, None] == segs[None, :]) & (index[:, None] >= index[None, :])
    return (jnp.cos(angle), jnp.sin(angle), visible)


def apply_rotary(tensor, cosine_table, sine_table, sign):
    half = tensor.shape[-1] // 2
    first = tensor[..., :half]
    second = tensor[..., half:]
    cos_b = cosine_table[:, None, :]
    sin_b = sine_table[:, None, :] * sign
    return jnp.concatenate(
        [first * cos_b - second * sin_b, second * cos_b + first * sin_b], axis=-1
    )


def norm_fwd(rows, gain):
    recip = lax.rsqrt(jnp.mean(rows * rows, axis=1, keepdims=True) + EPS)
    normal = rows * recip
    return ((normal * gain.astype(F32)).astype(BF), normal, recip)


def norm_bwd(upper, normal, recip, gain):
    dgain = jnp.sum(upper * normal, axis=0)
    scaled = upper * gain.astype(F32)
    return (dgain, recip * (scaled - normal * jnp.mean(scaled * normal, axis=1, keepdims=True)))


def after(value, *deps):
    return lax.optimization_barrier((value,) + deps)[0]


def make_body(S, R):
    C = 2
    n = R // C
    assert S % 2 == 0 and R % C == 0 and (n == 1 or n % 2 == 0)
    H = S // C
    both = ("shard", "rep")

    def peer(a, k):
        return lax.ppermute(a, "shard", [(i, i ^ k) for i in range(S)])

    def partner(a):
        return lax.ppermute(a, "rep", [(i, i ^ 1) for i in range(R)])

    def parity(a, even, odd):
        pairs = []
        for i in range(S):
            for j in range(R):
                pairs.append((i * R + j, (i ^ (even if j % 2 == 0 else odd)) * R + j))
        return lax.ppermute(a, both, pairs)

    def chips(a, pairs):
        return lax.ppermute(
            a, "rep", [(p * C + c, q * C + c) for p, q in pairs for c in range(C)]
        )

    def chain(part, zi):
        if n == 1:
            return part
        acc = part
        m = n // 2
        for i in range(m - 1):
            got = chips(acc, [(i, i + 1), (n - 1 - i, n - 2 - i)])
            acc = (acc.astype(F32) + got.astype(F32)).astype(BF)
        got = chips(acc, [(m - 1, m), (m, m - 1)])
        acc = (acc.astype(F32) + got.astype(F32)).astype(BF)
        for i in range(m - 2, -1, -1):
            got = chips(acc, [(i + 1, i), (n - 2 - i, n - 1 - i)])
            acc = jnp.where((zi == i) | (zi == n - 1 - i), got, acc)
        return acc

    def body(
        layer_in, segments, cotangent, w_query, key_matrix, value_matrix, output_matrix,
        gain_attn, w_gate, w_up, w_down, gain_ffn,
    ):
        T, D = layer_in.shape
        W = w_query.shape[0]
        FF = w_gate.shape[1]
        FS = FF // S
        QD = w_query.shape[1]
        KD = key_matrix.shape[1]
        QKV = QD + 2 * KD
        HB = min(W, (W // C + 15) // 16 * 16)
        HO = W - HB
        head_size = HEAD_WIDTH
        KV = KEY_VALUE_HEADS
        group = QUERY_HEADS // KV
        s = lax.axis_index("shard")
        r = lax.axis_index("rep")
        c = r % C
        zi = r // C
        z32 = jnp.int32(0)

        gains = jnp.stack([gain_attn, gain_ffn])
        gfull = jnp.zeros((2, D), BF)
        gfull = lax.dynamic_update_slice(gfull, gains, (z32, s * W))
        for k in range(1, S):
            gfull = lax.dynamic_update_slice(gfull, peer(gains, k), (z32, (s ^ k) * W))
        full_g1 = gfull[0]
        full_g2 = gfull[1]

        own_a = jnp.concatenate([w_query, key_matrix, value_matrix, output_matrix.T], axis=1)
        width = own_a.shape[1]
        half_a = lax.dynamic_slice(own_a, (c * HO, z32), (HB, width))
        if S == 4:
            got1 = parity(half_a, 1, 2)
            got2 = parity(jnp.stack([half_a, got1]), 2, 1)
            mine = [got1, got2[0], got2[1]]
            order = (1 + c, 2 - c, 3)
            other_order = (2 - c, 1 + c, 3)
        else:
            mine = [peer(half_a, k) for k in range(1, S)]
            order = other_order = tuple(range(1, S))
            got2 = mine[-1]
        other = partner(jnp.stack(mine))
        wa = jnp.zeros((D, width), BF)
        wa = lax.dynamic_update_slice(wa, own_a, (s * W, z32))
        for blk, k in zip(mine, order):
            wa = lax.dynamic_update_slice(wa, blk, ((s ^ k) * W + c * HO, z32))
        for i, k in enumerate(other_order):
            wa = lax.dynamic_update_slice(wa, other[i], ((s ^ k) * W + (1 - c) * HO, z32))
        w_qkv = wa[:, :QKV]
        w_ot = wa[:, QKV:]

        own_f = jnp.stack([w_gate, w_up, w_down.T])
        own_f = after(own_f, got2)
        fgot = []
        for k in range(1, S):
            fgot.append(
                peer(lax.dynamic_slice(own_f, (z32, c * HO, (s ^ k) * FS), (3, HB, FS)), k)
            )
        fother = partner(jnp.stack(fgot))
        wf = jnp.zeros((3, D, FS), BF)
        wf = lax.dynamic_update_slice(
            wf, lax.dynamic_slice(own_f, (z32, z32, s * FS), (3, W, FS)), (z32, s * W, z32)
        )
        for k in range(1, S):
            row = (s ^ k) * W
            wf = lax.dynamic_update_slice(wf, fgot[k - 1], (z32, row + c * HO, z32))
            wf = lax.dynamic_update_slice(wf, fother[k - 1], (z32, row + (1 - c) * HO, z32))
        wg, wu, wdt = wf[0], wf[1], wf[2]

        dout = cotangent.astype(BF)
        dout_s = after(dout, *fgot)
        doutg = jnp.concatenate([dout] + [peer(dout_s, k) for k in range(1, S)], axis=0)

        cosine_table, sine_table, visible = tables(segments, head_size)
        n1, xn1, recip1 = norm_fwd(layer_in, full_g1)
        qkv = matmul_plain(n1, w_qkv)
        qk = apply_rotary(
            qkv[:, : QD + KD].reshape(T, QUERY_HEADS + KV, head_size),
            cosine_table, sine_table, 1.0,
        ).astype(BF)
        query_rows = qk[:, :QUERY_HEADS].reshape(T, KV, group, head_size)
        key_rows = qk[:, QUERY_HEADS:]
        value_rows = qkv[:, QD + KD :].reshape(T, KV, head_size).astype(BF)
        raw = mixing("qhgd,khd->hgqk", query_rows, key_rows) * head_size ** (-0.5)
        logits = jnp.where(visible[None, None], raw, -1e30)
        peak = jnp.max(logits, axis=-1)
        lse = peak + jnp.log(jnp.sum(jnp.exp(logits - peak[..., None]), axis=-1))
        prob32 = jnp.exp(logits - lse[..., None])
        probs_b = prob32.astype(BF)
        attn = mixing("hgqk,khd->qhgd", probs_b, value_rows).reshape(T, QD).astype(BF)
        mid = layer_in + matmul_transposed(attn, w_ot)
        n2, xn2, recip2 = norm_fwd(mid, full_g2)

        n2g = jnp.concatenate([n2] + [peer(n2, k) for k in range(1, S)], axis=0)
        gate = matmul_plain(n2g, wg)
        upval = matmul_plain(n2g, wu)
        sigm = jax.nn.sigmoid(gate)
        silu = gate * sigm
        hidden = (silu * upval).astype(BF)
        dhid = matmul_plain(doutg, wdt)
        dgate = (dhid * upval * sigm * (1.0 + gate * (1.0 - sigm))).astype(BF)
        dup = (dhid * silu).astype(BF)
        dn2p = matmul_transposed(dgate, wg) + matmul_transposed(dup, wu)
        dn2pb = dn2p.astype(BF)
        dn2got = [peer(dn2pb[k * T : (k + 1) * T], k) for k in range(1, S)]
        dn2 = dn2p[:T]
        for g in dn2got:
            dn2 = dn2 + g.astype(F32)
        outp = matmul_transposed(hidden, wdt)
        outpb = outp.astype(BF)
        outpb = after(outpb, *dn2got)
        result = mid + outp[:T]
        for k in range(1, S):
            result = result + peer(outpb[k * T : (k + 1) * T], k).astype(F32)

        def reduce_core(g):
            rows = g.shape[0] // C
            send = lax.dynamic_slice(g, ((1 - c) * rows, z32), (rows, g.shape[1])).astype(BF)
            keep = lax.dynamic_slice(g, (c * rows, z32), (rows, g.shape[1]))
            return (keep + partner(send).astype(F32)).astype(BF)

        b = s % H
        back = []
        for j in range(H):
            pairs = []
            for si in range(S):
                for ri in range(R):
                    ci = ri % C
                    dst_s = H * ci + (j ^ (si % H))
                    dst_r = ri - ci + si // H
                    pairs.append((si * R + ri, dst_s * R + dst_r))
            back.append(pairs)

        def ffn_grad(left, right):
            part = reduce_core(dot_tn(left, right))
            tot = chain(part, zi).reshape(H, W, FS)
            q = []
            for j in range(H):
                blk = lax.dynamic_slice(tot, (j ^ b, z32, z32), (1, W, FS))[0]
                q.append(lax.ppermute(blk, both, back[j]))
            e = partner(jnp.stack(q))
            out = jnp.zeros((W, FF), F32)
            for j in range(H):
                out = lax.dynamic_update_slice(
                    out, q[j].astype(F32), (z32, (H * c + (j ^ b)) * FS)
                )
                out = lax.dynamic_update_slice(
                    out, e[j].astype(F32), (z32, (H * (1 - c) + (j ^ b)) * FS)
                )
            return out

        grad_gate = ffn_grad(n2g, dgate)
        grad_up = ffn_grad(n2g, dup)
        grad_down = ffn_grad(doutg, hidden).T

        g_gain2, dmid_n = norm_bwd(dn2, xn2, recip2, full_g2)
        dmid = cotangent + dmid_n

        dmid_b = dmid.astype(BF)

        def columns(a, k):
            return lax.dynamic_slice(a, (z32, (s ^ k) * W), (T, W))

        n1c = jnp.concatenate([columns(n1, 0)] + [peer(columns(n1, k), k) for k in range(1, S)])
        attng = jnp.concatenate([attn] + [peer(attn, k) for k in range(1, S)])
        dmidc = jnp.concatenate(
            [columns(dmid_b, 0)] + [peer(columns(dmid_b, k), k) for k in range(1, S)]
        )
        da = matmul_plain(dmid_b, w_ot).astype(BF).reshape(T, KV, group, head_size)
        value_gradient = mixing("hgqk,qhgd->khd", probs_b, da)
        dprob = mixing("qhgd,khd->hgqk", da, value_rows)
        delta = jnp.sum(prob32 * dprob, axis=-1)
        dscore = (prob32 * (dprob - delta[..., None]) * head_size ** (-0.5)).astype(BF)
        dquery = mixing("hgqk,khd->qhgd", dscore, key_rows).reshape(T, QUERY_HEADS, head_size)
        key_gradient = mixing("hgqk,qhgd->khd", dscore, query_rows)
        dqk = apply_rotary(
            jnp.concatenate([dquery, key_gradient], axis=1), cosine_table, sine_table, -1.0
        )
        dqkv = jnp.concatenate([dqk, value_gradient], axis=1).reshape(T, QKV).astype(BF)
        dqkvg = jnp.concatenate([dqkv] + [peer(dqkv, k) for k in range(1, S)])
        dn1 = matmul_transposed(dqkv, w_qkv)
        g_gain1, dx_n = norm_bwd(dn1, xn1, recip1, full_g1)
        input_grad = dmid + dx_n

        gg = jnp.stack([g_gain1, g_gain2])
        gsum = lax.dynamic_slice(gg, (z32, s * W), (2, W))
        for k in range(1, S):
            gsum = gsum + peer(lax.dynamic_slice(gg, (z32, (s ^ k) * W), (2, W)), k)
        grow = jnp.zeros((2 * HB - W, width), F32)
        grow = lax.dynamic_update_slice(grow, gsum.reshape(1, 2 * W), (z32, z32))
        ga = jnp.concatenate(
            [jnp.concatenate([dot_tn(n1c, dqkvg), dot_tn(dmidc, attng)], axis=1), grow]
        )
        ta = chain(reduce_core(ga), zi)
        tb = partner(ta)
        low = jnp.where(c == 0, ta, tb)
        high = jnp.where(c == 0, tb, ta)
        tot = jnp.concatenate([low, high]).astype(F32)
        return (
            result,
            input_grad,
            tot[:W, :QD],
            tot[:W, QD : QD + KD],
            tot[:W, QD + KD : QKV],
            tot[:W, QKV:].T,
            tot[W, :W],
            grad_gate,
            grad_up,
            grad_down,
            tot[W, W : 2 * W],
        )

    return body


def solution(mesh):
    return jax.shard_map(
        make_body(mesh.shape["shard"], mesh.shape["rep"]),
        mesh=mesh,
        in_specs=(
            P(("shard", "rep"), None),
            P(("shard", "rep")),
            P(("shard", "rep"), None),
            P("shard", None),
            P("shard", None),
            P("shard", None),
            P(None, "shard"),
            P("shard"),
            P("shard", None),
            P("shard", None),
            P(None, "shard"),
            P("shard"),
        ),
        out_specs=(
            P(("shard", "rep"), None),
            P(("shard", "rep"), None),
            P("shard", None),
            P("shard", None),
            P("shard", None),
            P(None, "shard"),
            P("shard"),
            P("shard", None),
            P("shard", None),
            P(None, "shard"),
            P("shard"),
        ),
        check_vma=False,
    )
```

```python
import jax
import jax.numpy as jnp
from jax import lax
from jax.experimental import pallas as pl
from jax.experimental.pallas import tpu as pltpu
from jax.sharding import PartitionSpec as P


QUERY_HEADS = 15
KEY_VALUE_HEADS = 5
HEAD_WIDTH = 64

EPS = 1e-05
THETA = 10000.0
BF = jnp.bfloat16
SH = "shard"
RP = "rep"
F32 = jnp.float32


def tables(segs, head_size):
    token_count = segs.shape[0]
    index = jnp.arange(token_count, dtype=jnp.int32)
    start = jnp.sum((segs[None, :] < segs[:, None]).astype(jnp.int32), axis=1)
    posit = (index - start).astype(F32)
    half = head_size // 2
    lane = jnp.arange(2 * head_size, dtype=jnp.int32)
    inverse = THETA ** (-(2.0 * (lane % half).astype(F32)) / head_size)
    angle = posit[:, None] * inverse[None, :]
    sign = jnp.where(lane % head_size < half, -1.0, 1.0)
    return (jnp.cos(angle), jnp.sin(angle) * sign[None, :])


def spot_of():
    return lax.axis_index(SH), lax.rem(lax.axis_index(RP), 2)


class Pieces:
    def __init__(self, own, mine, other, order, other_order, W, half, lead):
        self.own, self.mine, self.other = own, tuple(mine), tuple(other)
        self.order, self.other_order = order, other_order
        self.W, self.half, self.lead = W, half, lead

    def arrays(self):
        return (self.own,) + self.mine + self.other

    def count(self):
        return 1 + len(self.mine) + len(self.other)

    def jobs(self, refs, out_ref, pick=None):
        if pick is not None:
            refs = [ref.at[pick] for ref in refs]
        pre = (slice(None),) * self.lead
        if not self.mine:
            return [(refs[0], out_ref)]
        s, c = spot_of()
        W, half = self.W, self.half
        rest = W - half
        n = len(self.mine)

        def rows(at, size):
            return pre + (pl.ds(pl.multiple_of(at, 16), size),)

        jobs = [(refs[0], out_ref.at[rows(s * W, W)])]
        for i in range(n):
            row = (s ^ self.order[i](c)) * W + c * rest
            jobs.append((refs[1 + i], out_ref.at[rows(row, half)]))
        for i in range(n):
            row = (s ^ self.other_order[i](c)) * W + (1 - c) * half
            src = refs[1 + n + i].at[rows((1 - c) * (2 * half - W), rest)]
            jobs.append((src, out_ref.at[rows(row, rest)]))
        return jobs


def start_all(jobs, sems):
    copies = [pltpu.make_async_copy(a, b, sems.at[i]) for i, (a, b) in enumerate(jobs)]
    for cp in copies:
        cp.start()
    return copies


VM = pl.BlockSpec(memory_space=pltpu.VMEM)
ANY = pl.BlockSpec(memory_space=pl.ANY)
SM = pl.BlockSpec(memory_space=pltpu.SMEM)


def estimate(flops, moved):
    return pl.CostEstimate(flops=flops, transcendentals=0, bytes_accessed=moved)


def pack_attention(w_query, key_t, value_t, w_out, half):
    W, QD = w_query.shape
    KD = key_t.shape[0]
    width = 2 * (QD + KD)

    def kernel(q_ref, k_ref, v_ref, o_ref, own_o, half_o):
        _, c = spot_of()
        own_o[:, :QD] = q_ref[...]
        own_o[:, QD : QD + KD] = k_ref[...].T
        own_o[:, QD + KD : 2 * QD + KD] = o_ref[...].T
        own_o[:, 2 * QD + KD :] = v_ref[...].T
        half_o[...] = own_o[pl.ds(pl.multiple_of(c * (W - half), 16), half), :]

    return pl.pallas_call(
        kernel,
        name="ka",
        out_shape=(
            jax.ShapeDtypeStruct((W, width), BF),
            jax.ShapeDtypeStruct((half, width), BF),
        ),
        in_specs=[VM] * 4,
        out_specs=(VM, VM),
        cost_estimate=estimate(0, 6 * W * width),
    )(w_query, key_t, value_t, w_out)


def pack_feed_forward(w_gate, w_up, down_t, half, parts):
    W, FF = w_gate.shape
    FS = FF // parts

    def kernel(g_ref, u_ref, d_ref, own_o, *outs):
        s, c = spot_of()
        rows = pl.ds(pl.multiple_of(c * (W - half), 16), half)
        for p in range(parts):
            col = pl.ds(pl.multiple_of((s ^ p) * FS, 128), FS)
            for i, ref in enumerate((g_ref, u_ref, d_ref)):
                if p == 0:
                    own_o[i] = ref[:, col]
                else:
                    outs[p - 1][i] = ref[rows, col]

    return pl.pallas_call(
        kernel,
        name="kf",
        out_shape=(jax.ShapeDtypeStruct((3, W, FS), BF),)
        + (jax.ShapeDtypeStruct((3, half, FS), BF),) * (parts - 1),
        in_specs=[VM] * 3,
        out_specs=(VM,) * parts,
        cost_estimate=estimate(0, 12 * W * FF),
    )(w_gate, w_up, down_t)


def split_rows(acc, send_o, keep_o, cols=slice(None)):
    _, c = spot_of()
    half = acc.shape[0] // 2
    keep_o[...] = acc[pl.ds(pl.multiple_of(c * half, 8), half), cols]
    send_o[...] = acc[pl.ds(pl.multiple_of((1 - c) * half, 8), half), cols].astype(BF)


def feed_forward_first(blocks, pieces, D, gap):
    T = blocks[0].shape[0]
    count = len(blocks)
    FS = pieces.own.shape[-1]
    step = 2 if count % 2 == 0 else 1
    n_w = pieces.count()

    def kernel(*refs):
        rows = refs[:count]
        hid_o, dg_o, du_o, send_o, keep_o, w, acc, sems = refs[count + n_w :]
        copies = start_all(pieces.jobs(refs[count : count + n_w], w), sems)
        for cp in copies:
            cp.wait()
        for b in range(0, count, step):
            x = jnp.concatenate([rows[b + i][:, :D] for i in range(step)], axis=0)
            d = jnp.concatenate([rows[b + i][:, gap : gap + D] for i in range(step)], axis=0)
            at = slice(b * T, (b + step) * T)
            gate = mm(x, w[0])
            up = mm(x, w[1])
            dhid = mm(d, w[2])
            sig = 1.0 / (1.0 + jnp.exp(-gate))
            silu = gate * sig
            hid_o[at, :] = (silu * up).astype(BF)
            dg_o[at, :] = (dhid * up * sig * (1.0 + gate * (1.0 - sig))).astype(BF)
            du_o[at, :] = (dhid * silu).astype(BF)
        d = jnp.concatenate([r[:, gap : gap + D] for r in rows], axis=0)
        acc[...] = mm(d, hid_o[...], TN)
        split_rows(acc, send_o, keep_o)

    return pl.pallas_call(
        kernel,
        name="k1",
        out_shape=(jax.ShapeDtypeStruct((T * count, FS), BF),) * 3
        + (jax.ShapeDtypeStruct((D // 2, FS), BF), jax.ShapeDtypeStruct((D // 2, FS), F32)),
        in_specs=[VM] * count + [ANY] * n_w,
        out_specs=(VM,) * 5,
        scratch_shapes=[
            pltpu.VMEM((3, D, FS), BF),
            pltpu.VMEM((D, FS), F32),
            pltpu.SemaphoreType.DMA((n_w,)),
        ],
        cost_estimate=estimate(8 * T * count * D * FS, 6 * D * FS),
    )(*blocks, *pieces.arrays())


def feed_forward_rest(blocks, left, right_w, pieces, pick, D):
    T = blocks[0].shape[0]
    count = len(blocks)
    FS = pieces.own.shape[-1]
    n_w = pieces.count()
    n_r = len(right_w)
    step = 2 if count % 2 == 0 else 1

    def kernel(*refs):
        rows = refs[:count]
        left_ref = refs[count]
        rw = refs[count + 1 : count + 1 + n_r]
        base = count + 1 + n_r
        send_o, keep_o, own_o = refs[base + n_w : base + n_w + 3]
        outs = refs[base + n_w + 3 : base + n_w + 2 + count]
        w, acc, sems = refs[base + n_w + 2 + count :]
        copies = start_all(pieces.jobs(refs[base : base + n_w], w, pick), sems)
        x = jnp.concatenate([r[:, :D] for r in rows], axis=0)
        acc[...] = mm(x, left_ref[...], TN)
        split_rows(acc, send_o, keep_o)
        for cp in copies:
            cp.wait()
        for b in range(0, count, step):
            at = slice(b * T, (b + step) * T)
            y = mm(rw[0][at, :], w[0], NT)
            for i in range(1, n_r):
                y = y + mm(rw[i][at, :], w[i], NT)
            for i in range(step):
                part = y[i * T : (i + 1) * T]
                if b + i == 0:
                    own_o[...] = part
                else:
                    outs[b + i - 1][...] = part.astype(BF)

    return pl.pallas_call(
        kernel,
        out_shape=(
            jax.ShapeDtypeStruct((D // 2, FS), BF),
            jax.ShapeDtypeStruct((D // 2, FS), F32),
            jax.ShapeDtypeStruct((T, D), F32),
        )
        + (jax.ShapeDtypeStruct((T, D), BF),) * (count - 1),
        in_specs=[VM] * (count + 1 + n_r) + [ANY] * n_w,
        out_specs=(VM,) * (2 + count),
        scratch_shapes=[
            pltpu.VMEM((n_r, D, FS), BF),
            pltpu.VMEM((D, FS), F32),
            pltpu.SemaphoreType.DMA((n_w,)),
        ],
        cost_estimate=estimate(2 * T * count * D * FS * (1 + n_r), 6 * D * FS),
    )(*blocks, left, *right_w, *pieces.arrays())


def place_columns(blocks, column_of):
    W, FS = blocks[0].shape
    count = len(blocks)
    full = FS * count

    def kernel(*refs):
        s, c = spot_of()
        for i in range(count):
            col = pl.ds(pl.multiple_of(column_of(i, s, c) * FS, 128), FS)
            refs[count][:, col] = refs[i][...].astype(F32)

    return pl.pallas_call(
        kernel,
        out_shape=jax.ShapeDtypeStruct((W, full), F32),
        in_specs=[VM] * count,
        out_specs=VM,
        cost_estimate=estimate(0, 6 * W * full),
    )(*blocks)


def attention_gradients(forward, backward, small, L, half):
    T, W, qk, QD, KD = L.T, L.W, L.qk, L.QD, L.KD
    count = len(forward)
    rows = 2 * half

    def kernel(*refs):
        fw = refs[:count]
        bw = refs[count : 2 * count]
        sm = refs[2 * count : 3 * count]
        send_o, keep_o, acc = refs[3 * count :]
        n1c = jnp.concatenate([r[:, QD:] for r in fw], axis=0)
        att = jnp.concatenate([r[:, :QD] for r in fw], axis=0)
        dqk = jnp.concatenate([r[:, :qk] for r in bw], axis=0)
        dv = jnp.concatenate([r[:, qk : qk + KD] for r in bw], axis=0)
        dmc = jnp.concatenate([r[:T, :] for r in sm], axis=0)
        low = W // 8 * 8
        acc[low:, :] = jnp.zeros((rows - low, L.width), F32)
        acc[:W, :qk] = mm(n1c, dqk, TN)
        acc[:W, qk : L.v0] = mm(dmc, att, TN)
        acc[:W, L.v0 :] = mm(n1c, dv, TN)
        gains = sm[0][T : T + 16, :].astype(F32)
        for r in sm[1:]:
            gains = gains + r[T : T + 16, :].astype(F32)
        acc[W : W + 2, :W] = gains[:2]
        split_rows(acc, send_o, keep_o)

    return pl.pallas_call(
        kernel,
        name="kg",
        out_shape=(
            jax.ShapeDtypeStruct((half, L.width), BF),
            jax.ShapeDtypeStruct((half, L.width), F32),
        ),
        in_specs=[VM] * (3 * count),
        out_specs=(VM, VM),
        scratch_shapes=[pltpu.VMEM((rows, L.width), F32)],
        cost_estimate=estimate(2 * W * L.width * T * count, 6 * half * L.width),
    )(*forward, *backward, *small)


def whole_rows(a_ref, b_ref):
    _, c = spot_of()
    a = a_ref[...].astype(F32)
    b = b_ref[...].astype(F32)
    low = jnp.where(c == 0, a, b)
    high = jnp.where(c == 0, b, a)
    return jnp.concatenate([low, high], axis=0)


def unpack_first(mine, other, W, QD, KD):
    def kernel(a_ref, b_ref, q_o, k_o, ga_o, gf_o):
        full = whole_rows(a_ref, b_ref)
        q_o[...] = full[:W, :QD]
        k_o[...] = full[:, QD:].T[:, :W]
        ga_o[...] = full[W : W + 1, :W]
        gf_o[...] = full[W + 1 : W + 2, :W]

    return pl.pallas_call(
        kernel,
        name="ku",
        out_shape=(
            jax.ShapeDtypeStruct((W, QD), F32),
            jax.ShapeDtypeStruct((KD, W), F32),
            jax.ShapeDtypeStruct((1, W), F32),
            jax.ShapeDtypeStruct((1, W), F32),
        ),
        in_specs=[VM, VM],
        out_specs=(VM,) * 4,
        cost_estimate=estimate(0, 6 * W * (QD + KD)),
    )(mine, other)


def unpack_second(mine, other, W, QD, KD):
    def kernel(a_ref, b_ref, o_o, v_o):
        full = whole_rows(a_ref, b_ref)
        o_o[...] = full[:, :QD].T[:, :W]
        v_o[...] = full[:, QD:].T[:, :W]

    return pl.pallas_call(
        kernel,
        name="kv",
        out_shape=(jax.ShapeDtypeStruct((QD, W), F32), jax.ShapeDtypeStruct((KD, W), F32)),
        in_specs=[VM, VM],
        out_specs=(VM,) * 2,
        cost_estimate=estimate(0, 6 * W * (QD + KD)),
    )(mine, other)


NT = (((1,), (1,)), ((), ()))
TN = (((0,), (0,)), ((), ()))
NN = (((1,), (0,)), ((), ()))


def mm(left, right, dims=NN):
    return lax.dot_general(left, right, dims, preferred_element_type=F32)


def swap_halves(tile):
    lane = lax.broadcasted_iota(jnp.int32, tile.shape, 1)
    low = lax.rem(lane, 64) < 32
    return jnp.where(low, pltpu.roll(tile, 96, 1), pltpu.roll(tile, 32, 1))


class Layout:
    def __init__(self, T, D, W, QD, KD):
        self.T, self.D, self.W, self.QD, self.KD = T, D, W, QD, KD
        self.qk = QD + KD
        self.v0 = self.qk + QD
        self.width = self.v0 + KD
        self.va = self.v0 // 128 * 128
        self.group = QUERY_HEADS // KEY_VALUE_HEADS


def group_rows(a, g, group):
    return jnp.concatenate(
        [a[:, HEAD_WIDTH * (group * g + i) : HEAD_WIDTH * (group * g + i + 1)] for i in range(group)],
        axis=0,
    )


def masked_scores(qg, kg, visible):
    return jnp.where(visible, mm(qg, kg, NT) * HEAD_WIDTH ** (-0.5), -1e30)


def probabilities(sc):
    peak = jnp.max(sc, axis=-1, keepdims=True)
    lse = peak + jnp.log(jnp.sum(jnp.exp(sc - peak), axis=-1, keepdims=True))
    return jnp.exp(sc - lse)


def visible_rows(segc, segr, T, group):
    row = lax.broadcasted_iota(jnp.int32, (T, T), 0)
    col = lax.broadcasted_iota(jnp.int32, (T, T), 1)
    vis = ((segc == segr) & (row >= col)).astype(F32)
    return jnp.concatenate([vis] * group, axis=0) > 0.5


def attention_forward(L, x, cot, cos, sin, segc, segr, g1, g2, pieces, gap):
    T, D = L.T, L.D
    S = D // L.W
    n_w = pieces.count()

    def kernel(x_ref, cot_ref, cos_ref, sin_ref, segc_ref, segr_ref, g1_ref, g2_ref, *rest):
        qkv_o, mid_o, n2_o = rest[n_w : n_w + 3]
        packs = rest[n_w + 3 : n_w + 3 + S]
        attn_o, w, sems = rest[n_w + 3 + S :]
        copies = start_all(pieces.jobs(rest[:n_w], w), sems)
        xv = x_ref[...].T
        xn = xv * lax.rsqrt(jnp.mean(xv * xv, axis=1, keepdims=True) + EPS)
        n1 = (xn * g1_ref[...].astype(F32)).astype(BF)
        n2_o[:, gap : gap + D] = cot_ref[...].T.astype(BF)
        write_columns(packs, n1, L.QD, L.W)
        vis = visible_rows(segc_ref[...], segr_ref[...], T, L.group)
        for cp in copies:
            cp.wait()
        for t in range(L.qk // 128):
            y = mm(n1, w[:, 128 * t : 128 * (t + 1)])
            y = y * cos_ref[...] + swap_halves(y) * sin_ref[...]
            qkv_o[:, 128 * t : 128 * (t + 1)] = y.astype(BF)
        vv = mm(n1, w[:, L.va :])[:, L.v0 - L.va :].astype(BF)
        qkv_o[:, L.qk :] = vv
        qk = qkv_o[:, : L.qk]
        for g in range(KEY_VALUE_HEADS):
            kg = qk[:, L.QD + HEAD_WIDTH * g : L.QD + HEAD_WIDTH * (g + 1)]
            vg = vv[:, HEAD_WIDTH * g : HEAD_WIDTH * (g + 1)]
            pr = probabilities(masked_scores(group_rows(qk, g, L.group), kg, vis))
            o = mm(pr.astype(BF), vg).astype(BF)
            for i in range(L.group):
                h = L.group * g + i
                attn_o[:, HEAD_WIDTH * h : HEAD_WIDTH * (h + 1)] = o[T * i : T * (i + 1)]
        att = attn_o[...]
        for pack in packs:
            pack[:, : L.QD] = att
        mid = xv + mm(att, w[:, L.qk : L.v0], NT)
        mid_o[...] = mid
        xn2 = mid * lax.rsqrt(jnp.mean(mid * mid, axis=1, keepdims=True) + EPS)
        n2_o[:, :D] = (xn2 * g2_ref[...].astype(F32)).astype(BF)

    return pl.pallas_call(
        kernel,
        name="kx",
        out_shape=(
            jax.ShapeDtypeStruct((T, L.qk + L.KD), BF),
            jax.ShapeDtypeStruct((T, D), F32),
            jax.ShapeDtypeStruct((T, gap + D), BF),
        )
        + (jax.ShapeDtypeStruct((T, L.QD + L.W), BF),) * S,
        in_specs=[VM] * 8 + [ANY] * n_w,
        out_specs=(VM,) * (3 + S),
        scratch_shapes=[
            pltpu.VMEM((T, L.QD), BF),
            pltpu.VMEM((D, L.width), BF),
            pltpu.SemaphoreType.DMA((n_w,)),
        ],
        cost_estimate=estimate(2 * T * D * L.width, 2 * D * L.width),
    )(x, cot, cos, sin, segc, segr, g1, g2, *pieces.arrays())


def slot_shift(slot, c, S):
    return (0, 1 + c, 2 - c, 3)[slot] if S == 4 else slot


def write_columns(packs, value, start, W, rows=slice(None)):
    s, c = spot_of()
    S = len(packs)
    for slot, pack in enumerate(packs):
        for j in range(S):

            @pl.when((s ^ slot_shift(slot, c, S)) == j)
            def _():
                pack[rows, start : start + W] = value[:, W * j : W * (j + 1)]


def attention_backward(
    L, x, mid, cot, dn2, dn2got, qkv, cos, sin, segc, segr, g1, g2, pieces
):
    T, D = L.T, L.D
    n_got = len(dn2got)
    n_w = pieces.count()
    S = D // L.W
    end = L.qk + L.KD

    def kernel(
        x_ref, mid_ref, cot_ref, qkv_ref, cos_ref, sin_ref, segc_ref, segr_ref, g1_ref,
        g2_ref, dn2_ref, *rest
    ):
        got_refs = rest[:n_got]
        packs = rest[n_got + n_w : n_got + n_w + S]
        dqkv_o, dx_o, w, dqk, da_s, sems = rest[n_got + n_w + S :]
        copies = start_all(pieces.jobs(rest[n_got : n_got + n_w], w), sems)
        head = slice(0, T)
        d2 = dn2_ref[...]
        for ref in got_refs:
            d2 = d2 + ref[...].astype(F32)
        mid = mid_ref[...]
        r2 = lax.rsqrt(jnp.mean(mid * mid, axis=1, keepdims=True) + EPS)
        xn2 = mid * r2
        gg2 = jnp.sum(d2 * xn2, axis=0, keepdims=True)
        e2 = d2 * g2_ref[...].astype(F32)
        dmid = cot_ref[...].T + r2 * (e2 - xn2 * jnp.mean(e2 * xn2, axis=1, keepdims=True))
        dmid_b = dmid.astype(BF)
        write_columns(packs, dmid_b, 0, L.W, head)
        vis = visible_rows(segc_ref[...], segr_ref[...], T, L.group)
        for cp in copies:
            cp.wait()
        da_s[...] = mm(dmid_b, w[:, L.qk : L.v0]).astype(BF)
        da = da_s[...]
        qk = qkv_ref[:, : L.qk]
        vv = qkv_ref[:, L.qk :]
        for g in range(KEY_VALUE_HEADS):
            cols = slice(HEAD_WIDTH * g, HEAD_WIDTH * (g + 1))
            kg = qk[:, L.QD + HEAD_WIDTH * g : L.QD + HEAD_WIDTH * (g + 1)]
            vg = vv[:, cols]
            qg = group_rows(qk, g, L.group)
            dg = group_rows(da, g, L.group)
            pr = probabilities(masked_scores(qg, kg, vis))
            dv = mm(pr.astype(BF), dg, TN)
            dp = mm(dg, vg, NT)
            delta = jnp.sum(pr * dp, axis=-1, keepdims=True)
            ds = (pr * (dp - delta) * HEAD_WIDTH ** (-0.5)).astype(BF)
            dq = mm(ds, kg)
            dk = mm(ds, qg, TN)
            for i in range(L.group):
                h = L.group * g + i
                dqk[:, HEAD_WIDTH * h : HEAD_WIDTH * (h + 1)] = dq[T * i : T * (i + 1)]
            dqk[:, L.QD + HEAD_WIDTH * g : L.QD + HEAD_WIDTH * (g + 1)] = dk
            dqk[:, L.qk + HEAD_WIDTH * g : L.qk + HEAD_WIDTH * (g + 1)] = dv
        for t in range(L.qk // 128):
            tile = slice(128 * t, 128 * (t + 1))
            y = dqk[:, tile]
            dqkv_o[:, tile] = (y * cos_ref[...] - swap_halves(y) * sin_ref[...]).astype(BF)
        dvb = dqk[:, L.qk :].astype(BF)
        dqkv_o[:, L.qk :] = dvb
        pad = jnp.concatenate([jnp.zeros((T, L.v0 - L.va), BF), dvb], axis=1)
        dn1 = mm(dqkv_o[:, : L.qk], w[:, : L.qk], NT) + mm(pad, w[:, L.va :], NT)
        xv = x_ref[...].T
        r1 = lax.rsqrt(jnp.mean(xv * xv, axis=1, keepdims=True) + EPS)
        xn1 = xv * r1
        gg1 = jnp.sum(dn1 * xn1, axis=0, keepdims=True)
        gg = jnp.concatenate([gg1, gg2, jnp.zeros((14, D), F32)], axis=0).astype(BF)
        tail = slice(T, T + 16)
        write_columns(packs, gg, 0, L.W, tail)
        e1 = dn1 * g1_ref[...].astype(F32)
        dx_o[...] = (dmid + r1 * (e1 - xn1 * jnp.mean(e1 * xn1, axis=1, keepdims=True))).T

    return pl.pallas_call(
        kernel,
        name="ky",
        out_shape=(jax.ShapeDtypeStruct((T + 16, L.W), BF),) * S
        + (jax.ShapeDtypeStruct((T, end), BF), jax.ShapeDtypeStruct((D, T), F32)),
        in_specs=[VM] * (11 + n_got) + [ANY] * n_w,
        out_specs=(VM,) * (S + 2),
        scratch_shapes=[
            pltpu.VMEM((D, L.width), BF),
            pltpu.VMEM((T, end), F32),
            pltpu.VMEM((T, L.QD), BF),
            pltpu.SemaphoreType.DMA((n_w,)),
        ],
        cost_estimate=estimate(2 * T * D * L.width, 2 * D * L.width),
    )(x, mid, cot, qkv, cos, sin, segc, segr, g1, g2, dn2, *dn2got, *pieces.arrays())


def make_body(S, R):
    C = 2
    n = R // C
    assert S % 2 == 0 and R % C == 0 and (n == 1 or n % 2 == 0)
    H = S // C
    both = (SH, RP)

    def peer(a, k):
        pairs = [(i, i ^ k) for i in range(S)]
        return lax.ppermute(a, SH, pairs)

    def partner(a):
        pairs = [(i, i ^ 1) for i in range(R)]
        return lax.ppermute(a, RP, pairs)

    def parity(a, even, odd):
        pairs = []
        for i in range(S):
            for j in range(R):
                pairs.append((i * R + j, (i ^ (even if j % 2 == 0 else odd)) * R + j))
        return lax.ppermute(a, both, pairs)

    def gather(a):
        if S != 4:
            return [peer(a, k) for k in range(1, S)]
        near = parity(a, 1, 2)
        return [near, parity(a, 2, 1), parity(near, 2, 1)]

    def hand_back(blocks):
        if S != 4:
            return [peer(a, k) for k, a in enumerate(blocks, 1)]
        return [parity(blocks[0], 1, 2), parity(blocks[1], 2, 1), peer(blocks[2], 3)]

    def chips(a, pairs):
        full = [(p * C + c, q * C + c) for p, q in pairs for c in range(C)]
        return lax.ppermute(a, RP, full)

    m = n // 2

    def add(a, b):
        return (a.astype(F32) + b.astype(F32)).astype(BF)

    def inward(part):
        acc = part
        for i in range(m - 1):
            got = chips(acc, [(i, i + 1), (n - 1 - i, n - 2 - i)])
            acc = add(acc, got)
        return acc

    def across(acc):
        if n == 1:
            return acc
        return add(acc, chips(acc, [(m - 1, m), (m, m - 1)]))

    def outward(acc, zi):
        for i in range(m - 2, -1, -1):
            got = chips(acc, [(i + 1, i), (n - 2 - i, n - 1 - i)])
            acc = jnp.where((zi == i) | (zi == n - 1 - i), got, acc)
        return acc

    def body(
        layer_in, segments, cotangent, w_query, key_matrix, value_matrix, output_matrix,
        gain_attn, w_gate, w_up, w_down, gain_ffn,
    ):
        T, D = layer_in.shape
        W = w_query.shape[0]
        FF = w_gate.shape[1]
        FS = FF // S
        QD = w_query.shape[1]
        KD = key_matrix.shape[1]
        HB = min(W, (W // C + 15) // 16 * 16)
        HO = W - HB
        head_size = HEAD_WIDTH
        s = lax.axis_index(SH)
        r = lax.axis_index(RP)
        c = r % C
        zi = r // C
        z32 = jnp.int32(0)

        gains = jnp.stack([gain_attn, gain_ffn])
        gfull = jnp.zeros((2, D), BF)
        gfull = lax.dynamic_update_slice(gfull, gains, (z32, s * W))
        for k in range(1, S):
            gfull = lax.dynamic_update_slice(gfull, peer(gains, k), (z32, (s ^ k) * W))

        aligned = W % 16 == 0 and HB % 16 == 0 and HO % 16 == 0 and FS % 128 == 0
        x_t = layer_in.T
        cot_t = cotangent.T

        L = Layout(T, D, W, QD, KD)
        width = L.width
        if aligned:
            own_a, half_a = pack_attention(
                w_query, key_matrix.T, value_matrix.T, output_matrix, HB
            )
        else:
            own_a = jnp.concatenate([w_query, key_matrix, output_matrix.T, value_matrix], axis=1)
            half_a = lax.dynamic_slice(own_a, (c * HO, z32), (HB, width))
        if S == 4:
            near = parity(half_a, 1, 2)
            far = parity(half_a, 2, 1)
            mine = [near, far, parity(near, 2, 1)]
            order = (lambda c: 1 + c, lambda c: 2 - c, lambda c: 3)
            other_order = (lambda c: 2 - c, lambda c: 1 + c, lambda c: 3)
        else:
            mine = [peer(half_a, k) for k in range(1, S)]
            order = other_order = tuple((lambda c, k=k: k) for k in range(1, S))
        other = [partner(a) for a in mine[:-1]] + [partner(mine[-1])]
        plain = tuple((lambda c, k=k: k) for k in range(1, S))

        def pieces_of(shape, lead, own, mine, other, order, other_order):
            if aligned:
                return Pieces(own, mine, other, order, other_order, W, HB, lead)
            zeros = (z32,) * lead
            full = jnp.zeros(shape, BF)
            full = lax.dynamic_update_slice(full, own, zeros + (s * W, z32))
            for blk, k in zip(mine, order):
                row = (s ^ k(c)) * W + c * HO
                full = lax.dynamic_update_slice(full, blk, zeros + (row, z32))
            for blk, k in zip(other, other_order):
                row = (s ^ k(c)) * W + (1 - c) * HO
                full = lax.dynamic_update_slice(full, blk, zeros + (row, z32))
            return Pieces(full, (), (), (), (), W, HB, lead)

        pieces_a = pieces_of((D, width), 0, own_a, mine, other, order, other_order)

        peers = tuple(range(1, S))
        if aligned:
            packed = pack_feed_forward(w_gate, w_up, w_down.T, HB, S)
            fown, fsend = packed[0], packed[1:]
        else:
            own_f = jnp.stack([w_gate, w_up, w_down.T])
            fown = lax.dynamic_slice(own_f, (z32, z32, s * FS), (3, W, FS))
            fsend = [
                lax.dynamic_slice(own_f, (z32, c * HO, (s ^ k) * FS), (3, HB, FS)) for k in peers
            ]
        fgot = [peer(fsend[k - 1], k) for k in peers]
        fother = [partner(a) for a in fgot]
        pieces_f = pieces_of((3, D, FS), 1, fown, fgot, fother, plain, plain)

        cos_t, sin_t = tables(segments, head_size)
        segc = segments[:, None]
        segr = segments[None, :]
        g1row = gfull[0:1]
        g2row = gfull[1:2]
        gap = (D + 127) // 128 * 128
        qkv, mid, n2d, *fpack = attention_forward(
            L, x_t, cot_t, cos_t, sin_t, segc, segr, g1row, g2row, pieces_a, gap
        )

        blocks = [n2d] + gather(n2d)
        fgot_pack = [fpack[0]] + hand_back(fpack[1:])

        def reduce_split(send, keep):
            got = partner(send)
            return (keep + got.astype(F32)).astype(BF)

        hidden, dgate, dup, gd_send, gd_keep = feed_forward_first(blocks, pieces_f, D, gap)
        part1 = reduce_split(gd_send, gd_keep)
        gg_send, gg_keep, dn2_own, *dn2_out = feed_forward_rest(
            blocks, dgate, (dgate, dup), pieces_f, slice(0, 2), D
        )
        part2 = reduce_split(gg_send, gg_keep)
        dn2got = hand_back(dn2_out)
        gu_send, gu_keep, outp_own, *outp_out = feed_forward_rest(
            blocks, dup, (hidden,), pieces_f, slice(2, 3), D
        )
        part3 = reduce_split(gu_send, gu_keep)
        in1 = inward(part1)
        in2 = inward(part2)
        in3 = inward(part3)

        b = s % H
        back = []
        for j in range(H):
            pairs = []
            for si in range(S):
                for ri in range(R):
                    ci = ri % C
                    dst_s = H * ci + (j ^ (si % H))
                    dst_r = ri - ci + si // H
                    pairs.append((si * R + ri, dst_s * R + dst_r))
            back.append(pairs)

        def to_owner(tot):
            tot = tot.reshape(H, W, FS)
            q = []
            for j in range(H):
                blk = lax.dynamic_slice(tot, (j ^ b, z32, z32), (1, W, FS))[0]
                q.append(lax.ppermute(blk, both, back[j]))
            e = [partner(a) for a in q]

            def column_of(i, s, c):
                near = c if i < H else 1 - c
                return H * near + ((i % H) ^ lax.rem(s, H))

            if aligned:
                return place_columns(q + e, column_of)
            out = jnp.zeros((W, FF), F32)
            for i, blk in enumerate(q + e):
                at = column_of(i, s, c) * FS
                out = lax.dynamic_update_slice(out, blk.astype(F32), (z32, at))
            return out

        sum1 = across(in1)
        sum2 = across(in2)
        sum3 = across(in3)
        tot1 = outward(sum1, zi)
        tot2 = outward(sum2, zi)
        tot3 = outward(sum3, zi)

        *bpack, dqkv, dx_t = attention_backward(
            L, x_t, mid, cot_t, dn2_own, dn2got, qkv, cos_t, sin_t, segc, segr,
            g1row, g2row, pieces_a,
        )
        bgot = [dqkv] + gather(dqkv)
        small = [bpack[0]] + hand_back(bpack[1:])
        out_got = hand_back(outp_out)
        result = mid + outp_own
        for got in out_got:
            result = result + got.astype(F32)
        ga_send, ga_keep = attention_gradients(fgot_pack, bgot, small, L, HB)
        ga_got = partner(ga_send)

        def part_of(cols):
            return (ga_keep[:, cols] + ga_got[:, cols].astype(F32)).astype(BF)

        in4 = inward(part_of(slice(0, L.qk)))
        in5 = inward(part_of(slice(L.qk, None)))
        sum4 = across(in4)
        sum5 = across(in5)
        tot4 = outward(sum4, zi)
        tot5 = outward(sum5, zi)
        grad_down = to_owner(tot1).T
        grad_gate = to_owner(tot2)
        grad_up = to_owner(tot3)
        grad_q, grad_k_t, gain1_g, gain2_g = unpack_first(tot4, partner(tot4), W, QD, KD)
        grad_out, grad_v_t = unpack_second(tot5, partner(tot5), W, QD, KD)
        return (
            result,
            dx_t.T,
            grad_q,
            grad_k_t.T,
            grad_v_t.T,
            grad_out,
            gain1_g[0],
            grad_gate,
            grad_up,
            grad_down,
            gain2_g[0],
        )

    return body


def solution(mesh):
    return jax.shard_map(
        make_body(mesh.shape[SH], mesh.shape[RP]),
        mesh=mesh,
        in_specs=(
            P((SH, RP), None),
            P((SH, RP)),
            P((SH, RP), None),
            P(SH, None),
            P(SH, None),
            P(SH, None),
            P(None, SH),
            P(SH),
            P(SH, None),
            P(SH, None),
            P(None, SH),
            P(SH),
        ),
        out_specs=(
            P((SH, RP), None),
            P((SH, RP), None),
            P(SH, None),
            P(SH, None),
            P(SH, None),
            P(None, SH),
            P(SH),
            P(SH, None),
            P(SH, None),
            P(None, SH),
            P(SH),
        ),
        check_vma=False,
    )
```

```python
import jax
import jax.numpy as jnp
from jax import lax
from jax.experimental import pallas as pl
from jax.experimental.pallas import tpu as pltpu
from jax.sharding import PartitionSpec as P


QUERY_HEADS = 15
KEY_VALUE_HEADS = 5
HEAD_WIDTH = 64

EPS = 1e-05
THETA = 10000.0
BF = jnp.bfloat16
SH = "shard"
RP = "rep"
F32 = jnp.float32


def tables(segs, head_size):
    token_count = segs.shape[0]
    index = jnp.arange(token_count, dtype=jnp.int32)
    start = jnp.sum((segs[None, :] < segs[:, None]).astype(jnp.int32), axis=1)
    posit = (index - start).astype(F32)
    half = head_size // 2
    lane = jnp.arange(2 * head_size, dtype=jnp.int32)
    inverse = THETA ** (-(2.0 * (lane % half).astype(F32)) / head_size)
    angle = posit[:, None] * inverse[None, :]
    sign = jnp.where(lane % head_size < half, -1.0, 1.0)
    return (jnp.cos(angle), jnp.sin(angle) * sign[None, :])


def spot_of():
    return lax.axis_index(SH), lax.rem(lax.axis_index(RP), 2)


class Pieces:
    def __init__(self, own, mine, other, order, other_order, W, half, lead):
        self.own, self.mine, self.other = own, tuple(mine), tuple(other)
        self.order, self.other_order = order, other_order
        self.W, self.half, self.lead = W, half, lead

    def arrays(self):
        return (self.own,) + self.mine + self.other

    def count(self):
        return 1 + len(self.mine) + len(self.other)

    def jobs(self, refs, out_ref, pick=None):
        if pick is not None:
            refs = [ref.at[pick] for ref in refs]
        pre = (slice(None),) * self.lead
        if not self.mine:
            return [(refs[0], out_ref)]
        s, c = spot_of()
        W, half = self.W, self.half
        rest = W - half
        n = len(self.mine)

        def rows(at, size):
            return pre + (pl.ds(pl.multiple_of(at, 16), size),)

        jobs = [(refs[0], out_ref.at[rows(s * W, W)])]
        for i in range(n):
            row = (s ^ self.order[i](c)) * W + c * rest
            jobs.append((refs[1 + i], out_ref.at[rows(row, half)]))
        for i in range(n):
            row = (s ^ self.other_order[i](c)) * W + (1 - c) * half
            src = refs[1 + n + i].at[rows((1 - c) * (2 * half - W), rest)]
            jobs.append((src, out_ref.at[rows(row, rest)]))
        return jobs


def start_all(jobs, sems):
    copies = [pltpu.make_async_copy(a, b, sems.at[i]) for i, (a, b) in enumerate(jobs)]
    for cp in copies:
        cp.start()
    return copies


VM = pl.BlockSpec(memory_space=pltpu.VMEM)
ANY = pl.BlockSpec(memory_space=pl.ANY)
SM = pl.BlockSpec(memory_space=pltpu.SMEM)


def estimate(flops, moved):
    return pl.CostEstimate(flops=flops, transcendentals=0, bytes_accessed=moved)


def pack_attention(w_query, key_t, value_t, w_out, half):
    W, QD = w_query.shape
    KD = key_t.shape[0]
    width = 2 * (QD + KD)

    def kernel(q_ref, k_ref, v_ref, o_ref, own_o, half_o):
        _, c = spot_of()
        own_o[:, :QD] = q_ref[...]
        own_o[:, QD : QD + KD] = k_ref[...].T
        own_o[:, QD + KD : 2 * QD + KD] = o_ref[...].T
        own_o[:, 2 * QD + KD :] = v_ref[...].T
        half_o[...] = own_o[pl.ds(pl.multiple_of(c * (W - half), 16), half), :]

    return pl.pallas_call(
        kernel,
        name="ka",
        out_shape=(
            jax.ShapeDtypeStruct((W, width), BF),
            jax.ShapeDtypeStruct((half, width), BF),
        ),
        in_specs=[VM] * 4,
        out_specs=(VM, VM),
        cost_estimate=estimate(0, 6 * W * width),
    )(w_query, key_t, value_t, w_out)


def pack_feed_forward(w_gate, w_up, down_t, half, parts):
    W, FF = w_gate.shape
    FS = FF // parts

    def kernel(g_ref, u_ref, d_ref, own_o, *outs):
        s, c = spot_of()
        rows = pl.ds(pl.multiple_of(c * (W - half), 16), half)
        for p in range(parts):
            col = pl.ds(pl.multiple_of((s ^ p) * FS, 128), FS)
            for i, ref in enumerate((g_ref, u_ref, d_ref)):
                if p == 0:
                    own_o[i] = ref[:, col]
                else:
                    outs[p - 1][i] = ref[rows, col]

    return pl.pallas_call(
        kernel,
        name="kf",
        out_shape=(jax.ShapeDtypeStruct((3, W, FS), BF),)
        + (jax.ShapeDtypeStruct((3, half, FS), BF),) * (parts - 1),
        in_specs=[VM] * 3,
        out_specs=(VM,) * parts,
        cost_estimate=estimate(0, 12 * W * FF),
    )(w_gate, w_up, down_t)


def split_rows(acc, send_o, keep_o, cols=slice(None)):
    _, c = spot_of()
    half = acc.shape[0] // 2
    keep_o[...] = acc[pl.ds(pl.multiple_of(c * half, 8), half), cols]
    send_o[...] = acc[pl.ds(pl.multiple_of((1 - c) * half, 8), half), cols].astype(BF)


def feed_forward_first(blocks, pieces, D, gap):
    T = blocks[0].shape[0]
    count = len(blocks)
    FS = pieces.own.shape[-1]
    step = 2 if count % 2 == 0 else 1
    n_w = pieces.count()

    def kernel(*refs):
        rows = refs[:count]
        hid_o, dg_o, du_o, send_o, keep_o, w, acc, sems = refs[count + n_w :]
        copies = start_all(pieces.jobs(refs[count : count + n_w], w), sems)
        for cp in copies:
            cp.wait()
        for b in range(0, count, step):
            x = jnp.concatenate([rows[b + i][:, :D] for i in range(step)], axis=0)
            d = jnp.concatenate([rows[b + i][:, gap : gap + D] for i in range(step)], axis=0)
            at = slice(b * T, (b + step) * T)
            gate = mm(x, w[0])
            up = mm(x, w[1])
            dhid = mm(d, w[2])
            sig = 1.0 / (1.0 + jnp.exp(-gate))
            silu = gate * sig
            hid_o[at, :] = (silu * up).astype(BF)
            dg_o[at, :] = (dhid * up * sig * (1.0 + gate * (1.0 - sig))).astype(BF)
            du_o[at, :] = (dhid * silu).astype(BF)
        d = jnp.concatenate([r[:, gap : gap + D] for r in rows], axis=0)
        acc[...] = mm(d, hid_o[...], TN)
        split_rows(acc, send_o, keep_o)

    return pl.pallas_call(
        kernel,
        name="k1",
        out_shape=(jax.ShapeDtypeStruct((T * count, FS), BF),) * 3
        + (jax.ShapeDtypeStruct((D // 2, FS), BF), jax.ShapeDtypeStruct((D // 2, FS), F32)),
        in_specs=[VM] * count + [ANY] * n_w,
        out_specs=(VM,) * 5,
        scratch_shapes=[
            pltpu.VMEM((3, D, FS), BF),
            pltpu.VMEM((D, FS), F32),
            pltpu.SemaphoreType.DMA((n_w,)),
        ],
        cost_estimate=estimate(8 * T * count * D * FS, 6 * D * FS),
    )(*blocks, *pieces.arrays())


def feed_forward_rest(blocks, left, right_w, pieces, pick, D):
    T = blocks[0].shape[0]
    count = len(blocks)
    FS = pieces.own.shape[-1]
    n_w = pieces.count()
    n_r = len(right_w)
    step = 2 if count % 2 == 0 else 1

    def kernel(*refs):
        rows = refs[:count]
        left_ref = refs[count]
        rw = refs[count + 1 : count + 1 + n_r]
        base = count + 1 + n_r
        send_o, keep_o, own_o = refs[base + n_w : base + n_w + 3]
        outs = refs[base + n_w + 3 : base + n_w + 2 + count]
        w, acc, sems = refs[base + n_w + 2 + count :]
        copies = start_all(pieces.jobs(refs[base : base + n_w], w, pick), sems)
        x = jnp.concatenate([r[:, :D] for r in rows], axis=0)
        acc[...] = mm(x, left_ref[...], TN)
        split_rows(acc, send_o, keep_o)
        for cp in copies:
            cp.wait()
        for b in range(0, count, step):
            at = slice(b * T, (b + step) * T)
            y = mm(rw[0][at, :], w[0], NT)
            for i in range(1, n_r):
                y = y + mm(rw[i][at, :], w[i], NT)
            for i in range(step):
                part = y[i * T : (i + 1) * T]
                if b + i == 0:
                    own_o[...] = part
                else:
                    outs[b + i - 1][...] = part.astype(BF)

    return pl.pallas_call(
        kernel,
        out_shape=(
            jax.ShapeDtypeStruct((D // 2, FS), BF),
            jax.ShapeDtypeStruct((D // 2, FS), F32),
            jax.ShapeDtypeStruct((T, D), F32),
        )
        + (jax.ShapeDtypeStruct((T, D), BF),) * (count - 1),
        in_specs=[VM] * (count + 1 + n_r) + [ANY] * n_w,
        out_specs=(VM,) * (2 + count),
        scratch_shapes=[
            pltpu.VMEM((n_r, D, FS), BF),
            pltpu.VMEM((D, FS), F32),
            pltpu.SemaphoreType.DMA((n_w,)),
        ],
        cost_estimate=estimate(2 * T * count * D * FS * (1 + n_r), 6 * D * FS),
    )(*blocks, left, *right_w, *pieces.arrays())


def place_columns(blocks, column_of):
    W, FS = blocks[0].shape
    count = len(blocks)
    full = FS * count

    def kernel(*refs):
        s, c = spot_of()
        out_ref, narrow, wide, in_sems, out_sems = refs[count:]
        ins = start_all([(refs[i], narrow.at[i]) for i in range(count)], in_sems)
        outs = []
        for i in range(count):
            ins[i].wait()
            wide[i] = narrow[i].astype(F32)
            col = pl.ds(pl.multiple_of(column_of(i, s, c) * FS, 128), FS)
            outs.append(pltpu.make_async_copy(wide.at[i], out_ref.at[:, col], out_sems.at[i]))
            outs[i].start()
        for cp in outs:
            cp.wait()

    return pl.pallas_call(
        kernel,
        out_shape=jax.ShapeDtypeStruct((W, full), F32),
        in_specs=[ANY] * count,
        out_specs=ANY,
        scratch_shapes=[
            pltpu.VMEM((count, W, FS), BF),
            pltpu.VMEM((count, W, FS), F32),
            pltpu.SemaphoreType.DMA((count,)),
            pltpu.SemaphoreType.DMA((count,)),
        ],
        cost_estimate=estimate(0, 6 * W * full),
    )(*blocks)


def add_turned(first, second, others):
    T, D = first.shape

    def kernel(*refs):
        total = refs[0][...] + refs[1][...]
        for ref in refs[2:-1]:
            total = total + ref[...].astype(F32)
        refs[-1][...] = total.T

    return pl.pallas_call(
        kernel,
        name="kr",
        out_shape=jax.ShapeDtypeStruct((D, T), F32),
        in_specs=[VM] * (2 + len(others)),
        out_specs=VM,
        cost_estimate=estimate(0, 16 * T * D),
    )(first, second, *others)


def attention_gradients(forward, backward, small, L, half):
    T, W, qk, QD, KD = L.T, L.W, L.qk, L.QD, L.KD
    count = len(forward)
    rows = 2 * half

    def kernel(*refs):
        fw = refs[:count]
        bw = refs[count : 2 * count]
        sm = refs[2 * count : 3 * count]
        send_o, keep_o, acc = refs[3 * count :]
        n1c = jnp.concatenate([r[:, QD:] for r in fw], axis=0)
        att = jnp.concatenate([r[:, :QD] for r in fw], axis=0)
        dqk = jnp.concatenate([r[:, :qk] for r in bw], axis=0)
        dv = jnp.concatenate([r[:, qk : qk + KD] for r in bw], axis=0)
        dmc = jnp.concatenate([r[:T, :] for r in sm], axis=0)
        low = W // 8 * 8
        acc[low:, :] = jnp.zeros((rows - low, L.width), F32)
        acc[:W, :qk] = mm(n1c, dqk, TN)
        acc[:W, qk : L.v0] = mm(dmc, att, TN)
        acc[:W, L.v0 :] = mm(n1c, dv, TN)
        gains = sm[0][T : T + 16, :].astype(F32)
        for r in sm[1:]:
            gains = gains + r[T : T + 16, :].astype(F32)
        acc[W : W + 2, :W] = gains[:2]
        split_rows(acc, send_o, keep_o)

    return pl.pallas_call(
        kernel,
        name="kg",
        out_shape=(
            jax.ShapeDtypeStruct((half, L.width), BF),
            jax.ShapeDtypeStruct((half, L.width), F32),
        ),
        in_specs=[VM] * (3 * count),
        out_specs=(VM, VM),
        scratch_shapes=[pltpu.VMEM((rows, L.width), F32)],
        cost_estimate=estimate(2 * W * L.width * T * count, 6 * half * L.width),
    )(*forward, *backward, *small)


def whole_rows(a_ref, b_ref):
    _, c = spot_of()
    a = a_ref[...].astype(F32)
    b = b_ref[...].astype(F32)
    low = jnp.where(c == 0, a, b)
    high = jnp.where(c == 0, b, a)
    return jnp.concatenate([low, high], axis=0)


def unpack_first(mine, other, W, QD, KD):
    def kernel(a_ref, b_ref, q_o, k_o, ga_o, gf_o):
        full = whole_rows(a_ref, b_ref)
        q_o[...] = full[:W, :QD]
        k_o[...] = full[:, QD:].T[:, :W]
        ga_o[...] = full[W : W + 1, :W]
        gf_o[...] = full[W + 1 : W + 2, :W]

    return pl.pallas_call(
        kernel,
        name="ku",
        out_shape=(
            jax.ShapeDtypeStruct((W, QD), F32),
            jax.ShapeDtypeStruct((KD, W), F32),
            jax.ShapeDtypeStruct((1, W), F32),
            jax.ShapeDtypeStruct((1, W), F32),
        ),
        in_specs=[VM, VM],
        out_specs=(VM,) * 4,
        cost_estimate=estimate(0, 6 * W * (QD + KD)),
    )(mine, other)


def unpack_second(mine, other, W, QD, KD):
    def kernel(a_ref, b_ref, o_o, v_o):
        full = whole_rows(a_ref, b_ref)
        o_o[...] = full[:, :QD].T[:, :W]
        v_o[...] = full[:, QD:].T[:, :W]

    return pl.pallas_call(
        kernel,
        name="kv",
        out_shape=(jax.ShapeDtypeStruct((QD, W), F32), jax.ShapeDtypeStruct((KD, W), F32)),
        in_specs=[VM, VM],
        out_specs=(VM,) * 2,
        cost_estimate=estimate(0, 6 * W * (QD + KD)),
    )(mine, other)


NT = (((1,), (1,)), ((), ()))
TN = (((0,), (0,)), ((), ()))
NN = (((1,), (0,)), ((), ()))


def mm(left, right, dims=NN):
    return lax.dot_general(left, right, dims, preferred_element_type=F32)


def swap_halves(tile):
    lane = lax.broadcasted_iota(jnp.int32, tile.shape, 1)
    low = lax.rem(lane, 64) < 32
    return jnp.where(low, pltpu.roll(tile, 96, 1), pltpu.roll(tile, 32, 1))


class Layout:
    def __init__(self, T, D, W, QD, KD):
        self.T, self.D, self.W, self.QD, self.KD = T, D, W, QD, KD
        self.qk = QD + KD
        self.v0 = self.qk + QD
        self.width = self.v0 + KD
        self.va = self.v0 // 128 * 128
        self.group = QUERY_HEADS // KEY_VALUE_HEADS


def group_rows(a, g, group):
    return jnp.concatenate(
        [a[:, HEAD_WIDTH * (group * g + i) : HEAD_WIDTH * (group * g + i + 1)] for i in range(group)],
        axis=0,
    )


def masked_scores(qg, kg, visible):
    return jnp.where(visible, mm(qg, kg, NT) * HEAD_WIDTH ** (-0.5), -1e30)


def probabilities(sc):
    peak = jnp.max(sc, axis=-1, keepdims=True)
    lse = peak + jnp.log(jnp.sum(jnp.exp(sc - peak), axis=-1, keepdims=True))
    return jnp.exp(sc - lse)


def visible_rows(segc, segr, T, group):
    row = lax.broadcasted_iota(jnp.int32, (T, T), 0)
    col = lax.broadcasted_iota(jnp.int32, (T, T), 1)
    vis = ((segc == segr) & (row >= col)).astype(F32)
    return jnp.concatenate([vis] * group, axis=0) > 0.5


def attention_forward(L, x, cot, cos, sin, segc, segr, g1, g2, pieces, gap):
    T, D = L.T, L.D
    S = D // L.W
    n_w = pieces.count()

    def kernel(x_ref, cot_ref, cos_ref, sin_ref, segc_ref, segr_ref, g1_ref, g2_ref, *rest):
        qkv_o, mid_o, n2_o = rest[n_w : n_w + 3]
        packs = rest[n_w + 3 : n_w + 3 + S]
        attn_o, w, sems = rest[n_w + 3 + S :]
        copies = start_all(pieces.jobs(rest[:n_w], w), sems)
        xv = x_ref[...].T
        xn = xv * lax.rsqrt(jnp.mean(xv * xv, axis=1, keepdims=True) + EPS)
        n1 = (xn * g1_ref[...].astype(F32)).astype(BF)
        n2_o[:, gap : gap + D] = cot_ref[...].T.astype(BF)
        write_columns(packs, n1, L.QD, L.W)
        vis = visible_rows(segc_ref[...], segr_ref[...], T, L.group)
        for cp in copies:
            cp.wait()
        for t in range(L.qk // 128):
            y = mm(n1, w[:, 128 * t : 128 * (t + 1)])
            y = y * cos_ref[...] + swap_halves(y) * sin_ref[...]
            qkv_o[:, 128 * t : 128 * (t + 1)] = y.astype(BF)
        vv = mm(n1, w[:, L.va :])[:, L.v0 - L.va :].astype(BF)
        qkv_o[:, L.qk :] = vv
        qk = qkv_o[:, : L.qk]
        for g in range(KEY_VALUE_HEADS):
            kg = qk[:, L.QD + HEAD_WIDTH * g : L.QD + HEAD_WIDTH * (g + 1)]
            vg = vv[:, HEAD_WIDTH * g : HEAD_WIDTH * (g + 1)]
            pr = probabilities(masked_scores(group_rows(qk, g, L.group), kg, vis))
            o = mm(pr.astype(BF), vg).astype(BF)
            for i in range(L.group):
                h = L.group * g + i
                attn_o[:, HEAD_WIDTH * h : HEAD_WIDTH * (h + 1)] = o[T * i : T * (i + 1)]
        att = attn_o[...]
        for pack in packs:
            pack[:, : L.QD] = att
        mid = xv + mm(att, w[:, L.qk : L.v0], NT)
        mid_o[...] = mid
        xn2 = mid * lax.rsqrt(jnp.mean(mid * mid, axis=1, keepdims=True) + EPS)
        n2_o[:, :D] = (xn2 * g2_ref[...].astype(F32)).astype(BF)

    return pl.pallas_call(
        kernel,
        name="kx",
        out_shape=(
            jax.ShapeDtypeStruct((T, L.qk + L.KD), BF),
            jax.ShapeDtypeStruct((T, D), F32),
            jax.ShapeDtypeStruct((T, gap + D), BF),
        )
        + (jax.ShapeDtypeStruct((T, L.QD + L.W), BF),) * S,
        in_specs=[VM] * 8 + [ANY] * n_w,
        out_specs=(VM,) * (3 + S),
        scratch_shapes=[
            pltpu.VMEM((T, L.QD), BF),
            pltpu.VMEM((D, L.width), BF),
            pltpu.SemaphoreType.DMA((n_w,)),
        ],
        cost_estimate=estimate(2 * T * D * L.width, 2 * D * L.width),
    )(x, cot, cos, sin, segc, segr, g1, g2, *pieces.arrays())


def slot_shift(slot, c, S):
    return (0, 1 + c, 2 - c, 3)[slot] if S == 4 else slot


def write_columns(packs, value, start, W, rows=slice(None)):
    s, c = spot_of()
    S = len(packs)
    for slot, pack in enumerate(packs):
        for j in range(S):

            @pl.when((s ^ slot_shift(slot, c, S)) == j)
            def _():
                pack[rows, start : start + W] = value[:, W * j : W * (j + 1)]


def attention_backward(
    L, x, mid, cot, dn2, dn2got, qkv, cos, sin, segc, segr, g1, g2, pieces
):
    T, D = L.T, L.D
    n_got = len(dn2got)
    n_w = pieces.count()
    S = D // L.W
    end = L.qk + L.KD

    def kernel(
        x_ref, mid_ref, cot_ref, qkv_ref, cos_ref, sin_ref, segc_ref, segr_ref, g1_ref,
        g2_ref, dn2_ref, *rest
    ):
        got_refs = rest[:n_got]
        packs = rest[n_got + n_w : n_got + n_w + S]
        dqkv_o, dx_o, w, dqk, da_s, sems = rest[n_got + n_w + S :]
        copies = start_all(pieces.jobs(rest[n_got : n_got + n_w], w), sems)
        head = slice(0, T)
        d2 = dn2_ref[...]
        for ref in got_refs:
            d2 = d2 + ref[...].astype(F32)
        mid = mid_ref[...]
        r2 = lax.rsqrt(jnp.mean(mid * mid, axis=1, keepdims=True) + EPS)
        xn2 = mid * r2
        gg2 = jnp.sum(d2 * xn2, axis=0, keepdims=True)
        e2 = d2 * g2_ref[...].astype(F32)
        dmid = cot_ref[...].T + r2 * (e2 - xn2 * jnp.mean(e2 * xn2, axis=1, keepdims=True))
        dmid_b = dmid.astype(BF)
        write_columns(packs, dmid_b, 0, L.W, head)
        vis = visible_rows(segc_ref[...], segr_ref[...], T, L.group)
        for cp in copies:
            cp.wait()
        da_s[...] = mm(dmid_b, w[:, L.qk : L.v0]).astype(BF)
        da = da_s[...]
        qk = qkv_ref[:, : L.qk]
        vv = qkv_ref[:, L.qk :]
        for g in range(KEY_VALUE_HEADS):
            cols = slice(HEAD_WIDTH * g, HEAD_WIDTH * (g + 1))
            kg = qk[:, L.QD + HEAD_WIDTH * g : L.QD + HEAD_WIDTH * (g + 1)]
            vg = vv[:, cols]
            qg = group_rows(qk, g, L.group)
            dg = group_rows(da, g, L.group)
            pr = probabilities(masked_scores(qg, kg, vis))
            dv = mm(pr.astype(BF), dg, TN)
            dp = mm(dg, vg, NT)
            delta = jnp.sum(pr * dp, axis=-1, keepdims=True)
            ds = (pr * (dp - delta) * HEAD_WIDTH ** (-0.5)).astype(BF)
            dq = mm(ds, kg)
            dk = mm(ds, qg, TN)
            for i in range(L.group):
                h = L.group * g + i
                dqk[:, HEAD_WIDTH * h : HEAD_WIDTH * (h + 1)] = dq[T * i : T * (i + 1)]
            dqk[:, L.QD + HEAD_WIDTH * g : L.QD + HEAD_WIDTH * (g + 1)] = dk
            dqk[:, L.qk + HEAD_WIDTH * g : L.qk + HEAD_WIDTH * (g + 1)] = dv
        for t in range(L.qk // 128):
            tile = slice(128 * t, 128 * (t + 1))
            y = dqk[:, tile]
            dqkv_o[:, tile] = (y * cos_ref[...] - swap_halves(y) * sin_ref[...]).astype(BF)
        dvb = dqk[:, L.qk :].astype(BF)
        dqkv_o[:, L.qk :] = dvb
        pad = jnp.concatenate([jnp.zeros((T, L.v0 - L.va), BF), dvb], axis=1)
        dn1 = mm(dqkv_o[:, : L.qk], w[:, : L.qk], NT) + mm(pad, w[:, L.va :], NT)
        xv = x_ref[...].T
        r1 = lax.rsqrt(jnp.mean(xv * xv, axis=1, keepdims=True) + EPS)
        xn1 = xv * r1
        gg1 = jnp.sum(dn1 * xn1, axis=0, keepdims=True)
        gg = jnp.concatenate([gg1, gg2, jnp.zeros((14, D), F32)], axis=0).astype(BF)
        tail = slice(T, T + 16)
        write_columns(packs, gg, 0, L.W, tail)
        e1 = dn1 * g1_ref[...].astype(F32)
        dx_o[...] = (dmid + r1 * (e1 - xn1 * jnp.mean(e1 * xn1, axis=1, keepdims=True))).T

    return pl.pallas_call(
        kernel,
        name="ky",
        out_shape=(jax.ShapeDtypeStruct((T + 16, L.W), BF),) * S
        + (jax.ShapeDtypeStruct((T, end), BF), jax.ShapeDtypeStruct((D, T), F32)),
        in_specs=[VM] * (11 + n_got) + [ANY] * n_w,
        out_specs=(VM,) * (S + 2),
        scratch_shapes=[
            pltpu.VMEM((D, L.width), BF),
            pltpu.VMEM((T, end), F32),
            pltpu.VMEM((T, L.QD), BF),
            pltpu.SemaphoreType.DMA((n_w,)),
        ],
        cost_estimate=estimate(2 * T * D * L.width, 2 * D * L.width),
    )(x, mid, cot, qkv, cos, sin, segc, segr, g1, g2, dn2, *dn2got, *pieces.arrays())


def make_body(S, R):
    C = 2
    n = R // C
    assert S % 2 == 0 and R % C == 0 and (n == 1 or n % 2 == 0)
    H = S // C
    both = (SH, RP)

    def peer(a, k):
        pairs = [(i, i ^ k) for i in range(S)]
        return lax.ppermute(a, SH, pairs)

    def partner(a):
        pairs = [(i, i ^ 1) for i in range(R)]
        return lax.ppermute(a, RP, pairs)

    def parity(a, even, odd):
        pairs = []
        for i in range(S):
            for j in range(R):
                pairs.append((i * R + j, (i ^ (even if j % 2 == 0 else odd)) * R + j))
        return lax.ppermute(a, both, pairs)

    def gather(a):
        if S != 4:
            return [peer(a, k) for k in range(1, S)]
        near = parity(a, 1, 2)
        return [near, parity(a, 2, 1), parity(near, 2, 1)]

    def hand_back(blocks):
        if S != 4:
            return [peer(a, k) for k, a in enumerate(blocks, 1)]
        return [parity(blocks[0], 1, 2), parity(blocks[1], 2, 1), peer(blocks[2], 3)]

    def chips(a, pairs):
        full = [(p * C + c, q * C + c) for p, q in pairs for c in range(C)]
        return lax.ppermute(a, RP, full)

    m = n // 2

    def add(a, b):
        return (a.astype(F32) + b.astype(F32)).astype(BF)

    def inward(part):
        acc = part
        for i in range(m - 1):
            got = chips(acc, [(i, i + 1), (n - 1 - i, n - 2 - i)])
            acc = add(acc, got)
        return acc

    def across(acc):
        if n == 1:
            return acc
        return add(acc, chips(acc, [(m - 1, m), (m, m - 1)]))

    def outward(acc, zi):
        for i in range(m - 2, -1, -1):
            got = chips(acc, [(i + 1, i), (n - 2 - i, n - 1 - i)])
            acc = jnp.where((zi == i) | (zi == n - 1 - i), got, acc)
        return acc

    def body(
        layer_in, segments, cotangent, w_query, key_matrix, value_matrix, output_matrix,
        gain_attn, w_gate, w_up, w_down, gain_ffn,
    ):
        T, D = layer_in.shape
        W = w_query.shape[0]
        FF = w_gate.shape[1]
        FS = FF // S
        QD = w_query.shape[1]
        KD = key_matrix.shape[1]
        HB = min(W, (W // C + 15) // 16 * 16)
        HO = W - HB
        head_size = HEAD_WIDTH
        s = lax.axis_index(SH)
        r = lax.axis_index(RP)
        c = r % C
        zi = r // C
        z32 = jnp.int32(0)

        gains = jnp.stack([gain_attn, gain_ffn])
        gfull = jnp.zeros((2, D), BF)
        gfull = lax.dynamic_update_slice(gfull, gains, (z32, s * W))
        for k in range(1, S):
            gfull = lax.dynamic_update_slice(gfull, peer(gains, k), (z32, (s ^ k) * W))

        aligned = W % 16 == 0 and HB % 16 == 0 and HO % 16 == 0 and FS % 128 == 0
        x_t = layer_in.T
        cot_t = cotangent.T

        L = Layout(T, D, W, QD, KD)
        width = L.width
        if aligned:
            own_a, half_a = pack_attention(
                w_query, key_matrix.T, value_matrix.T, output_matrix, HB
            )
        else:
            own_a = jnp.concatenate([w_query, key_matrix, output_matrix.T, value_matrix], axis=1)
            half_a = lax.dynamic_slice(own_a, (c * HO, z32), (HB, width))
        if S == 4:
            near = parity(half_a, 1, 2)
            far = parity(half_a, 2, 1)
            mine = [near, far, parity(near, 2, 1)]
            order = (lambda c: 1 + c, lambda c: 2 - c, lambda c: 3)
            other_order = (lambda c: 2 - c, lambda c: 1 + c, lambda c: 3)
        else:
            mine = [peer(half_a, k) for k in range(1, S)]
            order = other_order = tuple((lambda c, k=k: k) for k in range(1, S))
        other = [partner(a) for a in mine[:-1]] + [partner(mine[-1])]
        plain = tuple((lambda c, k=k: k) for k in range(1, S))

        def pieces_of(shape, lead, own, mine, other, order, other_order):
            if aligned:
                return Pieces(own, mine, other, order, other_order, W, HB, lead)
            zeros = (z32,) * lead
            full = jnp.zeros(shape, BF)
            full = lax.dynamic_update_slice(full, own, zeros + (s * W, z32))
            for blk, k in zip(mine, order):
                row = (s ^ k(c)) * W + c * HO
                full = lax.dynamic_update_slice(full, blk, zeros + (row, z32))
            for blk, k in zip(other, other_order):
                row = (s ^ k(c)) * W + (1 - c) * HO
                full = lax.dynamic_update_slice(full, blk, zeros + (row, z32))
            return Pieces(full, (), (), (), (), W, HB, lead)

        pieces_a = pieces_of((D, width), 0, own_a, mine, other, order, other_order)

        peers = tuple(range(1, S))
        if aligned:
            packed = pack_feed_forward(w_gate, w_up, w_down.T, HB, S)
            fown, fsend = packed[0], packed[1:]
        else:
            own_f = jnp.stack([w_gate, w_up, w_down.T])
            fown = lax.dynamic_slice(own_f, (z32, z32, s * FS), (3, W, FS))
            fsend = [
                lax.dynamic_slice(own_f, (z32, c * HO, (s ^ k) * FS), (3, HB, FS)) for k in peers
            ]
        fgot = [peer(fsend[k - 1], k) for k in peers]
        fother = [partner(a) for a in fgot]
        pieces_f = pieces_of((3, D, FS), 1, fown, fgot, fother, plain, plain)

        cos_t, sin_t = tables(segments, head_size)
        segc = segments[:, None]
        segr = segments[None, :]
        g1row = gfull[0:1]
        g2row = gfull[1:2]
        gap = (D + 127) // 128 * 128
        qkv, mid, n2d, *fpack = attention_forward(
            L, x_t, cot_t, cos_t, sin_t, segc, segr, g1row, g2row, pieces_a, gap
        )

        blocks = [n2d] + gather(n2d)
        fgot_pack = [fpack[0]] + hand_back(fpack[1:])

        def reduce_split(send, keep):
            got = partner(send)
            return (keep + got.astype(F32)).astype(BF)

        hidden, dgate, dup, gd_send, gd_keep = feed_forward_first(blocks, pieces_f, D, gap)
        part1 = reduce_split(gd_send, gd_keep)
        gg_send, gg_keep, dn2_own, *dn2_out = feed_forward_rest(
            blocks, dgate, (dgate, dup), pieces_f, slice(0, 2), D
        )
        part2 = reduce_split(gg_send, gg_keep)
        dn2got = hand_back(dn2_out)
        gu_send, gu_keep, outp_own, *outp_out = feed_forward_rest(
            blocks, dup, (hidden,), pieces_f, slice(2, 3), D
        )
        part3 = reduce_split(gu_send, gu_keep)
        in1 = inward(part1)
        in2 = inward(part2)
        in3 = inward(part3)

        b = s % H
        back = []
        for j in range(H):
            pairs = []
            for si in range(S):
                for ri in range(R):
                    ci = ri % C
                    dst_s = H * ci + (j ^ (si % H))
                    dst_r = ri - ci + si // H
                    pairs.append((si * R + ri, dst_s * R + dst_r))
            back.append(pairs)

        def to_owner(tot):
            tot = tot.reshape(H, W, FS)
            q = []
            for j in range(H):
                blk = lax.dynamic_slice(tot, (j ^ b, z32, z32), (1, W, FS))[0]
                q.append(lax.ppermute(blk, both, back[j]))
            e = [partner(a) for a in q]

            def column_of(i, s, c):
                near = c if i < H else 1 - c
                return H * near + ((i % H) ^ lax.rem(s, H))

            if aligned:
                return place_columns(q + e, column_of)
            out = jnp.zeros((W, FF), F32)
            for i, blk in enumerate(q + e):
                at = column_of(i, s, c) * FS
                out = lax.dynamic_update_slice(out, blk.astype(F32), (z32, at))
            return out

        sum1 = across(in1)
        sum2 = across(in2)
        sum3 = across(in3)
        tot1 = outward(sum1, zi)
        tot2 = outward(sum2, zi)
        tot3 = outward(sum3, zi)

        *bpack, dqkv, dx_t = attention_backward(
            L, x_t, mid, cot_t, dn2_own, dn2got, qkv, cos_t, sin_t, segc, segr,
            g1row, g2row, pieces_a,
        )
        bgot = [dqkv] + gather(dqkv)
        small = [bpack[0]] + hand_back(bpack[1:])
        out_got = hand_back(outp_out)
        result_t = add_turned(mid, outp_own, out_got)
        ga_send, ga_keep = attention_gradients(fgot_pack, bgot, small, L, HB)
        ga_got = partner(ga_send)

        def part_of(cols):
            return (ga_keep[:, cols] + ga_got[:, cols].astype(F32)).astype(BF)

        in4 = inward(part_of(slice(0, L.qk)))
        in5 = inward(part_of(slice(L.qk, None)))
        sum4 = across(in4)
        sum5 = across(in5)
        tot4 = outward(sum4, zi)
        tot5 = outward(sum5, zi)
        grad_down = to_owner(tot1).T
        grad_gate = to_owner(tot2)
        grad_up = to_owner(tot3)
        grad_q, grad_k_t, gain1_g, gain2_g = unpack_first(tot4, partner(tot4), W, QD, KD)
        grad_out, grad_v_t = unpack_second(tot5, partner(tot5), W, QD, KD)
        return (
            result_t.T,
            dx_t.T,
            grad_q,
            grad_k_t.T,
            grad_v_t.T,
            grad_out,
            gain1_g[0],
            grad_gate,
            grad_up,
            grad_down,
            gain2_g[0],
        )

    return body


def solution(mesh):
    return jax.shard_map(
        make_body(mesh.shape[SH], mesh.shape[RP]),
        mesh=mesh,
        in_specs=(
            P((SH, RP), None),
            P((SH, RP)),
            P((SH, RP), None),
            P(SH, None),
            P(SH, None),
            P(SH, None),
            P(None, SH),
            P(SH),
            P(SH, None),
            P(SH, None),
            P(None, SH),
            P(SH),
        ),
        out_specs=(
            P((SH, RP), None),
            P((SH, RP), None),
            P(SH, None),
            P(SH, None),
            P(SH, None),
            P(None, SH),
            P(SH),
            P(SH, None),
            P(SH, None),
            P(None, SH),
            P(SH),
        ),
        check_vma=False,
    )
```
